32 devices in a mesh: band: 8 (over z, y), pair: 4 (over x, core).
Axes of the slice: x: 2, y: 2, z: 4, core: 2. Of those that a mesh axis runs over, the one named last changes fastest.
Arguments:
- orbitals: bfloat16 [32, 262144], P(('band', 'pair')), may hold values from -64 to 64
- partners: int32 [32, 3], P(('band', 'pair')), may hold values from -1 to 31, as said below
Outputs:
- gradient: float32 [32, 262144], P(None, ('band', 'pair'))
The draws below stay inside these ranges and needn't reach their ends.
Inputs may be any that keep to these rules, and one draw needn't show every extreme that they name: `partners`: slot k of orbital i holds either -1 or i XOR (4 * 2**k); j is listed by i exactly when i is listed by j.
All inputs are finite; a program needn't handle non-finite values.
Results may differ from the reference program's by a relative error of at most 0.0008.
The reference program's roundings to bfloat16 on the way (of `term` and `applied`) count: a program that leaves them out, or rounds other values in their place, can miss the bound.
Values may be sent and summed in bfloat16 or wider, within the bound.
A program may use at most 64 MiB of HBM per device.

```python
import math
import jax
import jax.numpy as jnp
from jax import lax

NG = 64
PARTNERS = 3
NG3 = 262144
ORBITALS = 32
N_PAIR = 4


def draw_orbitals(key, part):
    count = ORBITALS
    index = jnp.arange(count, dtype=jnp.int32)
    cluster = index // N_PAIR // 8
    clusters = count // (8 * N_PAIR)
    centers = jax.random.uniform(jax.random.fold_in(key, 11), (clusters, 3), jnp.float32, 0.25 * NG, 0.75 * NG)
    jitter = jax.random.uniform(jax.random.fold_in(key, 12), (count, 3), jnp.float32, -NG / 12.0, NG / 12.0)
    where = centers[cluster] + jitter
    width = jnp.full((count, 1), NG / 6.0, jnp.float32)
    rough = jnp.clip(jax.random.normal(jax.random.fold_in(key, 14), (count, NG3), jnp.float32), -4.0, 4.0)
    coord = jnp.arange(NG, dtype=jnp.float32)[None, :]
    along_x = jnp.exp(-(coord - where[:, 0:1]) ** 2 / (2.0 * width * width))
    along_y = jnp.exp(-(coord - where[:, 1:2]) ** 2 / (2.0 * width * width))
    along_z = jnp.exp(-(coord - where[:, 2:3]) ** 2 / (2.0 * width * width))
    envelope = along_x[:, :, None, None] * along_y[:, None, :, None] * along_z[:, None, None, :]
    height = (NG / (math.sqrt(math.pi) * width)) ** 1.5
    return (rough * envelope.reshape(count, NG3) * height).astype(jnp.bfloat16)


def draw_partners(key, part):
    count = ORBITALS
    index = jnp.arange(count, dtype=jnp.int32)
    columns = []
    for slot in range(PARTNERS):
        stride = N_PAIR * 2 ** slot
        lowest = index - index // stride % 2 * stride
        flags = jax.random.randint(jax.random.fold_in(key, 21 + slot), (count,), 0, 2)
        forced = jnp.logical_or(lowest % (count // 2) == 0, lowest >= count - 2 * stride)
        live = jnp.logical_or(flags[lowest] == 1, forced)
        mate = index + stride - 2 * (index // stride % 2) * stride
        columns.append(jnp.where(live, mate, -1))
    return jnp.stack(columns, axis=1).astype(jnp.int32)


def setup_inputs(seed: int = 0) -> dict:
    arg_keys = jax.random.split(jax.random.key(seed), 3)
    orbitals = draw_orbitals(jax.random.fold_in(arg_keys[2], 71), 0)
    partners = draw_partners(jax.random.fold_in(arg_keys[2], 71), 0)
    return {"orbitals": orbitals, "partners": partners}


screening = 0.05

def sine_table(size):
    index = jnp.arange(size, dtype=jnp.int32) + 1
    product = index[:, None] * index[None, :] % (2 * (size + 1))
    angle = math.pi * product.astype(jnp.float32) / (size + 1)
    return jnp.sqrt(jnp.float32(2.0 / (size + 1))) * jnp.sin(angle)

def eigen_sum(size):
    steps = jnp.arange(size, dtype=jnp.float32) + 1.0
    lam = 2.0 - 2.0 * jnp.cos(math.pi * steps / (size + 1))
    total = lam[:, None, None] + lam[None, :, None] + lam[None, None, :] + screening
    return total.reshape(size, size * size)

def sine_transform(field, table, doubled):
    size = table.shape[0]
    highest = lax.Precision.HIGHEST
    field = jnp.dot(table, field, precision=highest)
    field = jnp.dot(field.reshape(-1, 2 * size), doubled, precision=highest)
    field = jnp.einsum('ky,xyz->xkz', table, field.reshape(size, size, size), precision=highest)
    return field.reshape(size, size * size)

def screened_solve(density, table, doubled, denom):
    return sine_transform(sine_transform(density, table, doubled) / denom, table, doubled)

def reference(orbitals, partners):
    table = sine_table(NG)
    doubled = jnp.kron(jnp.eye(2, dtype=jnp.float32), table)
    denom = eigen_sum(NG)

    def apply_one(index):
        own = orbitals[index].reshape(NG, NG * NG).astype(jnp.float32)
        total = jnp.zeros((NG, NG * NG), jnp.float32)
        for slot in range(PARTNERS):
            other_index = partners[index, slot]
            other = orbitals[jnp.maximum(other_index, 0)].reshape(NG, NG * NG).astype(jnp.float32)
            potential = screened_solve(own * other, table, doubled, denom)
            term = lax.optimization_barrier((potential * other).astype(jnp.bfloat16))
            total = total + jnp.where(other_index >= 0, term.astype(jnp.float32), 0.0)
        return total.astype(jnp.bfloat16).reshape(NG3)
    applied = lax.map(apply_one, jnp.arange(ORBITALS, dtype=jnp.int32))
    intersection = lax.dot_general(orbitals, applied, (((1,), (1,)), ((), ())), preferred_element_type=jnp.float32)
    intersection = intersection * (1.0 / NG3)
    removed = lax.dot_general(intersection, orbitals.astype(jnp.float32), (((0,), (0,)), ((), ())), precision=lax.Precision.HIGHEST)
    return applied.astype(jnp.float32) - removed
```

```python
import functools

import jax
import jax.numpy as jnp
import numpy as np
from jax import lax
from jax.experimental import pallas as pl
from jax.experimental.pallas import tpu as pltpu
from jax.sharding import PartitionSpec as P

screening = 0.05
GROUP = 8
MESH = pl.DeviceIdType.MESH


def halves(table):
    high = table.astype(np.float32).astype(jnp.bfloat16)
    low = (table - high.astype(np.float64)).astype(jnp.bfloat16)
    return np.asarray(high), np.asarray(low)


def tables(size):
    index = np.arange(size) + 1
    product = index[:, None] * index[None, :] % (2 * (size + 1))
    sine = np.sqrt(2.0 / (size + 1)) * np.sin(np.pi * product / (size + 1))
    half = size // 2
    high, low = halves(sine)
    left = np.block([[high, high], [low, low]])
    high, low = halves(np.kron(np.eye(2), sine))
    right = np.block([[high, low], [high, low]])
    even, odd = sine[:half, 0::2], sine[:half, 1::2]
    high, low = halves(np.concatenate([even, odd], axis=1))
    forth = np.block([[high, high], [low, low]])
    high, low = halves(np.concatenate([even.T, odd.T], axis=1))
    back = np.block([[high, high], [low, low]])
    lam = 2.0 - 2.0 * np.cos(np.pi * index / (size + 1))
    pair = np.concatenate(
        [lam[:half, None] + lam[None, :], lam[::-1][:half, None] + lam[None, :]], axis=1
    )
    pair = (pair + screening).astype(np.float32)
    along = np.broadcast_to(lam.astype(np.float32)[:, None], (size, 2 * size)).copy()
    return left, right, forth, back, pair, along


def split(value, axis):
    high = value.astype(jnp.bfloat16)
    low = (value - high.astype(jnp.float32)).astype(jnp.bfloat16)
    return jnp.concatenate([high, low], axis=axis)


def dot(a, b):
    return jnp.dot(a, b, preferred_element_type=jnp.float32)


def stacked(value, lanes):
    return jnp.concatenate(
        [value[:, at : at + lanes] for at in range(0, value.shape[1], lanes)], axis=0
    )


def spread(value, rows):
    return jnp.concatenate(
        [value[at : at + rows] for at in range(0, value.shape[0], rows)], axis=1
    )


def solve(density, work, left, right, forth, back, pair, along):
    lanes = density.shape[1]
    size, half = lanes // 2, lanes // 4
    lane = lax.broadcasted_iota(jnp.int32, (half, GROUP * lanes), 1) % lanes
    first = lane < size
    sign = jnp.where(
        lax.broadcasted_iota(jnp.int32, (GROUP * half, lanes), 1) < size, 1.0, -1.0
    ).astype(jnp.float32)

    def planes(source, start):
        field = jnp.concatenate(
            [source[pl.ds(start + i, size, stride=half), :] for i in range(GROUP)], axis=1
        )
        field = dot(left[...], split(field, 0))
        field = stacked(field[:size] + field[size:], lanes)
        field = dot(split(field, 1), right[...])
        return field[:, :lanes] + field[:, lanes:]

    def middle(table, field):
        field = jnp.concatenate(
            [jnp.where(first, field, 0.0), jnp.where(first, 0.0, field)], axis=0
        )
        field = dot(table[...], split(field, 0))
        return stacked(field[:half] + field[half:], lanes)

    def fold(field):
        return pltpu.roll(field, size, 1) + field * sign

    for start in range(0, half, GROUP):
        work[start * size : (start + GROUP) * size, :] = planes(density, start)
    for start in range(0, size, GROUP):
        field = jnp.concatenate(
            [work[pl.ds(start + i, half, stride=size), :] for i in range(GROUP)], axis=1
        )
        field = fold(middle(forth, field))
        denom = jnp.concatenate(
            [pair[...] + along[start + i : start + i + 1, :] for i in range(GROUP)], axis=0
        )
        field = middle(back, spread(fold(field / denom), half))
        density[start * half : (start + GROUP) * half, :] = field
    for start in range(0, half, GROUP):
        field = planes(density, start)
        for i in range(GROUP):
            work[pl.ds(start + i, size, stride=half), :] = field[i * size : (i + 1) * size]


def slot_kernel(slot, last, live, own, other, *refs):
    earlier, refs = refs[: 2 * last], refs[2 * last :]
    left, right, forth, back, pair, along, out, density, work = refs

    @pl.when(live[slot] >= 0)
    def _():
        density[...] = own[...].astype(jnp.float32) * other[...].astype(jnp.float32)
        solve(density, work, left, right, forth, back, pair, along)
        term = (work[...] * other[...].astype(jnp.float32)).astype(jnp.bfloat16)
        if last:
            total = earlier[0][...].astype(jnp.float32) + earlier[1][...].astype(jnp.float32)
            term = (total + term.astype(jnp.float32)).astype(jnp.bfloat16)
        out[...] = term

    @pl.when(live[slot] < 0)
    def _():
        if last:
            total = earlier[0][...].astype(jnp.float32) + earlier[1][...].astype(jnp.float32)
            out[...] = total.astype(jnp.bfloat16)
        else:
            out[...] = jnp.zeros_like(out)


def slot_term(slot, live, own, other, earlier, consts):
    vmem = pl.BlockSpec(memory_space=pltpu.VMEM)
    rows, lanes = own.shape
    return pl.pallas_call(
        functools.partial(slot_kernel, slot, 1 if earlier else 0),
        out_shape=jax.ShapeDtypeStruct(own.shape, jnp.bfloat16),
        in_specs=[pl.BlockSpec(memory_space=pltpu.SMEM)] + [vmem] * (2 + len(earlier) + len(consts)),
        out_specs=vmem,
        scratch_shapes=[pltpu.VMEM((rows, lanes), jnp.float32)] * 2,
        cost_estimate=pl.CostEstimate(
            flops=24 * rows * lanes * lanes * 8, bytes_accessed=6 * rows * lanes, transcendentals=0
        ),
        name=f"slot{slot}",
    )(live, own, other, *earlier, *consts)


def place(index):
    pairs = lax.axis_size("pair")
    return (index // pairs, index % pairs)


def remove_kernel(count, cells, scale, applied, phi, out, slab, wide, sums, sent, came, sent2, came2, here):
    rows, lanes = slab.shape[1:]
    me = lax.axis_index("band") * lax.axis_size("pair") + lax.axis_index("pair")

    def regroup(step):
        peer = lax.rem(me + step, count)
        return pltpu.make_async_remote_copy(
            src_ref=applied.at[peer], dst_ref=slab.at[me], send_sem=sent.at[step],
            recv_sem=came.at[step], device_id=place(peer), device_id_type=MESH,
        )

    def share(step):
        peer = lax.rem(me + step, count)
        return pltpu.make_async_remote_copy(
            src_ref=sums.at[me], dst_ref=sums.at[me], send_sem=sent2.at[step],
            recv_sem=came2.at[step], device_id=place(peer), device_id_type=MESH,
        )

    def each(action):
        lax.fori_loop(1, count, lambda step, _: (action(step), 0)[1], 0)

    each(lambda step: regroup(step).start())
    own = pltpu.make_async_copy(applied.at[me], slab.at[me], here)
    own.start()
    own.wait()
    each(lambda step: regroup(step).wait())
    wide[...] = slab[...].reshape(count * rows, lanes).astype(jnp.float32)
    for row in range(rows):
        out[:, row * lanes : (row + 1) * lanes] = wide[pl.ds(row, count, stride=rows), :]
    partial = lax.dot_general(
        phi[...], out[...].astype(jnp.bfloat16), (((1,), (1,)), ((), ())),
        preferred_element_type=jnp.float32,
    ) * scale
    short = count * count // lanes
    sums[me] = jnp.concatenate(
        [partial[at : at + short] for at in range(0, count, short)], axis=1
    )
    each(lambda step: share(step).start())
    each(lambda step: share(step).wait())
    packed = jnp.sum(sums[...], axis=0)
    total = jnp.concatenate(
        [packed[:, at : at + count] for at in range(0, lanes, count)], axis=0
    )
    removed = lax.dot_general(
        total, phi[...].astype(jnp.float32), (((0,), (0,)), ((), ())),
        precision=lax.Precision.HIGHEST, preferred_element_type=jnp.float32,
    )
    out[...] = out[...] - removed


def regrouped(value, count):
    bands, pairs = lax.axis_size("band"), lax.axis_size("pair")
    rows, lanes = value.shape
    value = value.reshape(bands, pairs, rows // count, lanes)
    value = lax.all_to_all(value, "band", split_axis=0, concat_axis=0, tiled=True)
    value = lax.all_to_all(value, "pair", split_axis=1, concat_axis=1, tiled=True)
    return value.reshape(count, rows * lanes // count)


def on_device(orbitals, partners):
    cells = orbitals.shape[1]
    size = round(cells ** (1.0 / 3.0))
    lanes = 2 * size
    count = lax.axis_size("band") * lax.axis_size("pair")
    consts = [jnp.asarray(table) for table in tables(size)]
    own = orbitals.reshape(cells // lanes, lanes)
    live = partners[0]
    arrived = []
    for slot in range(partners.shape[1]):
        pairs = [(source, source ^ 2**slot) for source in range(lax.axis_size("band"))]
        arrived.append(lax.ppermute(own, "band", pairs))
    terms = []
    for slot in range(2):
        terms.append(slot_term(slot, live, own, arrived[slot], [], consts))
    applied = slot_term(2, live, own, arrived[2], terms, consts)
    phi = regrouped(own, count)
    scale = 1.0 / cells
    slab = cells // count
    if slab % (8 * lanes) or count * count % (8 * lanes):
        other = regrouped(applied, count)
        partial = lax.dot_general(
            phi, other, (((1,), (1,)), ((), ())), preferred_element_type=jnp.float32
        )
        total = lax.psum(partial * scale, ("band", "pair"))
    elif count * count * count * 4 > 2**24:
        other = regrouped(applied, count)
        partial = lax.dot_general(
            phi, other, (((1,), (1,)), ((), ())), preferred_element_type=jnp.float32
        )
        total = lax.psum(partial * scale, ("band", "pair"))
    else:
        vmem = pl.BlockSpec(memory_space=pltpu.VMEM)
        rows = slab // lanes
        return pl.pallas_call(
            functools.partial(remove_kernel, count, cells, scale),
            out_shape=jax.ShapeDtypeStruct((count, slab), jnp.float32),
            in_specs=[vmem, vmem],
            out_specs=vmem,
            scratch_shapes=[
                pltpu.VMEM((count, rows, lanes), jnp.bfloat16),
                pltpu.VMEM((count * rows, lanes), jnp.float32),
                pltpu.VMEM((count, count * count // lanes, lanes), jnp.float32),
                pltpu.SemaphoreType.DMA((count,)),
                pltpu.SemaphoreType.DMA((count,)),
                pltpu.SemaphoreType.DMA((count,)),
                pltpu.SemaphoreType.DMA((count,)),
                pltpu.SemaphoreType.DMA,
            ],
            compiler_params=pltpu.CompilerParams(has_side_effects=True),
            name="remove",
        )(applied.reshape(count, rows, lanes), phi)
    removed = lax.dot_general(
        total, phi.astype(jnp.float32), (((0,), (0,)), ((), ())), precision=lax.Precision.HIGHEST
    )
    return other.astype(jnp.float32) - removed


def solution(mesh):
    placed = (P(("band", "pair"), None), P(("band", "pair"), None))
    return jax.shard_map(
        on_device, mesh=mesh, in_specs=placed, out_specs=P(None, ("band", "pair")), check_vma=False
    )
```

```python
import functools

import jax
import jax.numpy as jnp
import numpy as np
from jax import lax
from jax.experimental import pallas as pl
from jax.experimental.pallas import tpu as pltpu
from jax.sharding import PartitionSpec as P

screening = 0.05
GROUP = 8
MESH = pl.DeviceIdType.MESH


def halves(table):
    high = table.astype(np.float32).astype(jnp.bfloat16)
    low = (table - high.astype(np.float64)).astype(jnp.bfloat16)
    return np.asarray(high), np.asarray(low)


def tables(size):
    index = np.arange(size) + 1
    product = index[:, None] * index[None, :] % (2 * (size + 1))
    sine = np.sqrt(2.0 / (size + 1)) * np.sin(np.pi * product / (size + 1))
    half = size // 2
    high, low = halves(sine)
    left = np.block([[high, high], [low, low]])
    high, low = halves(np.kron(np.eye(2), sine))
    right = np.block([[high, low], [high, low]])
    even, odd = sine[:half, 0::2], sine[:half, 1::2]
    high, low = halves(np.concatenate([even, odd], axis=1))
    forth = np.block([[high, high], [low, low]])
    high, low = halves(np.concatenate([even.T, odd.T], axis=1))
    back = np.block([[high, high], [low, low]])
    lam = 2.0 - 2.0 * np.cos(np.pi * index / (size + 1))
    pair = np.concatenate(
        [lam[:half, None] + lam[None, :], lam[::-1][:half, None] + lam[None, :]], axis=1
    )
    pair = (pair + screening).astype(np.float32)
    along = np.broadcast_to(lam.astype(np.float32)[:, None], (size, 2 * size)).copy()
    return left, right, forth, back, pair, along


def split(value, axis):
    high = value.astype(jnp.bfloat16)
    low = (value - high.astype(jnp.float32)).astype(jnp.bfloat16)
    return jnp.concatenate([high, low], axis=axis)


def dot(a, b):
    return jnp.dot(a, b, preferred_element_type=jnp.float32)


def stacked(value, lanes):
    return jnp.concatenate(
        [value[:, at : at + lanes] for at in range(0, value.shape[1], lanes)], axis=0
    )


def spread(value, rows):
    return jnp.concatenate(
        [value[at : at + rows] for at in range(0, value.shape[0], rows)], axis=1
    )


def middle(table, field, half):
    lanes = 4 * half
    lane = lax.broadcasted_iota(jnp.int32, field.shape, 1) % lanes
    first = lane < 2 * half
    field = jnp.concatenate([jnp.where(first, field, 0.0), jnp.where(first, 0.0, field)], axis=0)
    field = dot(table[...], split(field, 0))
    return stacked(field[:half] + field[half:], lanes)


def fold(field):
    size = field.shape[1] // 2
    sign = jnp.where(lax.broadcasted_iota(jnp.int32, field.shape, 1) < size, 1.0, -1.0)
    return pltpu.roll(field, size, 1) + field * sign.astype(jnp.float32)


def solve(own, other, work, consts):
    left, right, forth, back, pair, along = consts
    lanes = work.shape[1]
    size, half = lanes // 2, lanes // 4

    def across(field):
        field = dot(left[...], split(field, 0))
        return field[:size] + field[size:]

    def inner(field):
        field = dot(split(field, 1), right[...])
        return field[:, :lanes] + field[:, lanes:]

    for start in range(0, size, GROUP):
        rows = slice(start * half, (start + GROUP) * half)
        field = own[rows, :].astype(jnp.float32) * other[rows, :].astype(jnp.float32)
        work[rows, :] = fold(middle(forth, spread(field, half), half))
    for start in range(0, half, GROUP):
        field = jnp.concatenate(
            [work[pl.ds(start + i, size, stride=half), :] for i in range(GROUP)], axis=1
        )
        field = inner(stacked(across(field), lanes))
        denom = jnp.concatenate(
            [along[...] + pair[start + i : start + i + 1, :] for i in range(GROUP)], axis=0
        )
        field = across(spread(inner(field / denom), size))
        for i in range(GROUP):
            work[pl.ds(start + i, size, stride=half), :] = field[:, i * lanes : (i + 1) * lanes]


def finished(work, other, back, start):
    half = work.shape[1] // 4
    rows = slice(start * half, (start + GROUP) * half)
    field = middle(back, spread(fold(work[rows, :]), half), half)
    return rows, (field * other[rows, :].astype(jnp.float32)).astype(jnp.bfloat16)


def slot_kernel(slot, last, live, own, other, *refs):
    earlier, refs = refs[: 2 * last], refs[2 * last :]
    consts, out, work = refs[:6], refs[6], refs[7]
    solve(own, other, work, consts)
    for start in range(0, work.shape[1] // 2, GROUP):
        rows, term = finished(work, other, consts[3], start)
        term = jnp.where(live[slot] >= 0, term.astype(jnp.float32), 0.0)
        if last:
            total = earlier[0][rows, :].astype(jnp.float32) + earlier[1][rows, :].astype(jnp.float32)
            term = total + term
        out[rows, :] = term.astype(jnp.bfloat16)


def slot_term(slot, live, own, other, earlier, consts):
    vmem = pl.BlockSpec(memory_space=pltpu.VMEM)
    rows, lanes = own.shape
    return pl.pallas_call(
        functools.partial(slot_kernel, slot, 1 if earlier else 0),
        out_shape=jax.ShapeDtypeStruct(own.shape, jnp.bfloat16),
        in_specs=[pl.BlockSpec(memory_space=pltpu.SMEM)] + [vmem] * (2 + len(earlier) + len(consts)),
        out_specs=vmem,
        scratch_shapes=[pltpu.VMEM((rows, lanes), jnp.float32)],
        cost_estimate=pl.CostEstimate(
            flops=24 * rows * lanes * lanes * 8, bytes_accessed=6 * rows * lanes, transcendentals=0
        ),
        name=f"slot{slot}",
    )(live, own, other, *earlier, *consts)


def place(index):
    pairs = lax.axis_size("pair")
    return (index // pairs, index % pairs)


def whole_kernel(
    count, scale, live, orbital, *refs,
):
    consts, refs = refs[:6], refs[6:]
    out, own, other, terms, work, applied, slabs, phi, sums, slot_sems, sent, came = refs
    slots = other.shape[0]
    rows, lanes = slabs.shape[2:]
    band, pair = lax.axis_index("band"), lax.axis_index("pair")
    me = band * lax.axis_size("pair") + pair

    def each(action):
        lax.fori_loop(1, count, lambda step, _: (action(step), 0)[1], 0)

    def peer_of(step):
        return lax.rem(me + step, count)

    barrier = pltpu.get_barrier_semaphore()
    each(lambda step: pl.semaphore_signal(
        barrier, inc=1, device_id=place(peer_of(step)), device_id_type=MESH))
    grid = orbital[...].reshape(count * rows, lanes)
    own[...] = grid.reshape(count, rows, lanes)
    slabs[0, me] = own[me]
    pl.semaphore_wait(barrier, count - 1)

    def fetch(slot):
        stride = 2**slot
        mate = band + stride - 2 * stride * lax.rem(band // stride, 2)
        return pltpu.make_async_remote_copy(
            src_ref=own, dst_ref=other.at[slot], send_sem=slot_sems.at[0, slot],
            recv_sem=slot_sems.at[1, slot], device_id=(mate, pair), device_id_type=MESH,
        )

    def regroup(which, source):
        def copy(step):
            peer = peer_of(step)
            return pltpu.make_async_remote_copy(
                src_ref=source.at[peer], dst_ref=slabs.at[which, me],
                send_sem=sent.at[which, step], recv_sem=came.at[which, step],
                device_id=place(peer), device_id_type=MESH,
            )
        return copy

    def share(step):
        return pltpu.make_async_remote_copy(
            src_ref=sums.at[me], dst_ref=sums.at[me], send_sem=sent.at[2, step],
            recv_sem=came.at[2, step], device_id=place(peer_of(step)), device_id_type=MESH,
        )

    def widen(which):
        work[...] = slabs[which].reshape(count * rows, lanes).astype(jnp.float32)
        return [work[pl.ds(row, count, stride=rows), :] for row in range(rows)]

    fetches = [fetch(slot) for slot in range(slots)]
    for copy in fetches:
        copy.start()
    first, second = regroup(0, own), regroup(1, applied)
    each(lambda step: first(step).start())
    planes = lanes // 2
    flat = own.reshape(count * rows, lanes)
    for slot in range(slots):
        fetches[slot].wait()
        mate = other.at[slot].reshape(count * rows, lanes)
        solve(flat, mate, work, consts)
        for start in range(0, planes, GROUP):
            span, term = finished(work, mate, consts[3], start)
            term = jnp.where(live[0, slot] >= 0, term.astype(jnp.float32), 0.0)
            if slot + 1 < slots:
                terms[slot, span, :] = term.astype(jnp.bfloat16)
                continue
            total = terms[0, span, :].astype(jnp.float32)
            for earlier in range(1, slots - 1):
                total = total + terms[earlier, span, :].astype(jnp.float32)
            total = (total + term).astype(jnp.bfloat16)
            blocks = (span.stop - span.start) // rows
            at = span.start // rows
            applied[at : at + blocks] = total.reshape(blocks, rows, lanes)
    slabs[1, me] = applied[me]
    each(lambda step: second(step).start())
    each(lambda step: first(step).wait())
    for row, value in enumerate(widen(0)):
        phi[:, row * lanes : (row + 1) * lanes] = value.astype(jnp.bfloat16)
    each(lambda step: second(step).wait())
    for row, value in enumerate(widen(1)):
        out[:, row * lanes : (row + 1) * lanes] = value
    partial = lax.dot_general(
        phi[...], out[...].astype(jnp.bfloat16), (((1,), (1,)), ((), ())),
        preferred_element_type=jnp.float32,
    ) * scale
    short = count * count // lanes
    sums[me] = jnp.concatenate(
        [partial[at : at + short] for at in range(0, count, short)], axis=1
    )
    each(lambda step: share(step).start())
    each(lambda step: share(step).wait())
    packed = jnp.sum(sums[...], axis=0)
    total = jnp.concatenate(
        [packed[:, at : at + count] for at in range(0, lanes, count)], axis=0
    )
    removed = lax.dot_general(
        total, phi[...].astype(jnp.float32), (((0,), (0,)), ((), ())),
        precision=lax.Precision.HIGHEST, preferred_element_type=jnp.float32,
    )
    out[...] = out[...] - removed


def in_one_kernel(orbitals, partners, consts, count, lanes):
    cells = orbitals.shape[1]
    slots = partners.shape[1]
    slab = cells // count
    rows = slab // lanes
    vmem = pl.BlockSpec(memory_space=pltpu.VMEM)
    return pl.pallas_call(
        functools.partial(whole_kernel, count, 1.0 / cells),
        out_shape=jax.ShapeDtypeStruct((count, slab), jnp.float32),
        in_specs=[pl.BlockSpec(memory_space=pltpu.SMEM)] + [vmem] * (1 + len(consts)),
        out_specs=vmem,
        scratch_shapes=[
            pltpu.VMEM((count, rows, lanes), jnp.bfloat16),
            pltpu.VMEM((slots, count, rows, lanes), jnp.bfloat16),
            pltpu.VMEM((slots - 1, count * rows, lanes), jnp.bfloat16),
            pltpu.VMEM((count * rows, lanes), jnp.float32),
            pltpu.VMEM((count, rows, lanes), jnp.bfloat16),
            pltpu.VMEM((2, count, rows, lanes), jnp.bfloat16),
            pltpu.VMEM((count, slab), jnp.bfloat16),
            pltpu.VMEM((count, count * count // lanes, lanes), jnp.float32),
            pltpu.SemaphoreType.DMA((2, slots)),
            pltpu.SemaphoreType.DMA((3, count)),
            pltpu.SemaphoreType.DMA((3, count)),
        ],
        compiler_params=pltpu.CompilerParams(collective_id=0, has_side_effects=True),
        name="exchange",
    )(partners, orbitals, *consts)


def regrouped(value, count):
    bands, pairs = lax.axis_size("band"), lax.axis_size("pair")
    rows, lanes = value.shape
    value = value.reshape(bands, pairs, rows // count, lanes)
    value = lax.all_to_all(value, "band", split_axis=0, concat_axis=0, tiled=True)
    value = lax.all_to_all(value, "pair", split_axis=1, concat_axis=1, tiled=True)
    return value.reshape(count, rows * lanes // count)


def on_device(orbitals, partners):
    cells = orbitals.shape[1]
    size = round(cells ** (1.0 / 3.0))
    lanes = 2 * size
    count = lax.axis_size("band") * lax.axis_size("pair")
    consts = [jnp.asarray(table) for table in tables(size)]
    slab = cells // count
    small = count * count * count * 4 <= 2**24
    if small and slab % (8 * lanes) == 0 and count * count % (8 * lanes) == 0:
        return in_one_kernel(orbitals, partners, consts, count, lanes)
    own = orbitals.reshape(cells // lanes, lanes)
    live = partners[0]
    arrived = []
    for slot in range(partners.shape[1]):
        pairs = [(source, source ^ 2**slot) for source in range(lax.axis_size("band"))]
        arrived.append(lax.ppermute(own, "band", pairs))
    terms = []
    for slot in range(2):
        terms.append(slot_term(slot, live, own, arrived[slot], [], consts))
    applied = slot_term(2, live, own, arrived[2], terms, consts)
    phi, other = regrouped(own, count), regrouped(applied, count)
    partial = lax.dot_general(
        phi, other, (((1,), (1,)), ((), ())), preferred_element_type=jnp.float32
    )
    total = lax.psum(partial * (1.0 / cells), ("band", "pair"))
    removed = lax.dot_general(
        total, phi.astype(jnp.float32), (((0,), (0,)), ((), ())), precision=lax.Precision.HIGHEST
    )
    return other.astype(jnp.float32) - removed


def solution(mesh):
    placed = (P(("band", "pair"), None), P(("band", "pair"), None))
    return jax.shard_map(
        on_device, mesh=mesh, in_specs=placed, out_specs=P(None, ("band", "pair")), check_vma=False
    )
```

```python
import functools

import jax
import jax.numpy as jnp
import numpy as np
from jax import lax
from jax.experimental import pallas as pl
from jax.experimental.pallas import tpu as pltpu
from jax.sharding import PartitionSpec as P

screening = 0.05
GROUP = 8
CHUNKS = 4
MESH = pl.DeviceIdType.MESH


def halves(table):
    high = table.astype(np.float32).astype(jnp.bfloat16)
    low = (table - high.astype(np.float64)).astype(jnp.bfloat16)
    return np.asarray(high), np.asarray(low)


def tables(size):
    index = np.arange(size) + 1
    product = index[:, None] * index[None, :] % (2 * (size + 1))
    sine = np.sqrt(2.0 / (size + 1)) * np.sin(np.pi * product / (size + 1))
    half = size // 2
    high, low = halves(sine)
    left = np.block([[high, high], [low, low]])
    high, low = halves(np.kron(np.eye(2), sine))
    right = np.block([[high, low], [high, low]])
    even, odd = sine[:half, 0::2], sine[:half, 1::2]
    high, low = halves(np.concatenate([even, odd], axis=1))
    forth = np.block([[high, high], [low, low]])
    high, low = halves(np.concatenate([even.T, odd.T], axis=1))
    back = np.block([[high, high], [low, low]])
    lam = 2.0 - 2.0 * np.cos(np.pi * index / (size + 1))
    pair = np.concatenate(
        [lam[:half, None] + lam[None, :], lam[::-1][:half, None] + lam[None, :]], axis=1
    )
    pair = (pair + screening).astype(np.float32)
    along = np.broadcast_to(lam.astype(np.float32)[:, None], (size, 2 * size)).copy()
    return left, right, forth, back, pair, along


def split(value, axis):
    high = value.astype(jnp.bfloat16)
    low = (value - high.astype(jnp.float32)).astype(jnp.bfloat16)
    return jnp.concatenate([high, low], axis=axis)


def dot(a, b):
    return jnp.dot(a, b, preferred_element_type=jnp.float32)


def stacked(value, lanes):
    return jnp.concatenate(
        [value[:, at : at + lanes] for at in range(0, value.shape[1], lanes)], axis=0
    )


def spread(value, rows):
    return jnp.concatenate(
        [value[at : at + rows] for at in range(0, value.shape[0], rows)], axis=1
    )


def middle(table, field, half):
    lanes = 4 * half
    lane = lax.broadcasted_iota(jnp.int32, field.shape, 1) % lanes
    first = lane < 2 * half
    field = jnp.concatenate([jnp.where(first, field, 0.0), jnp.where(first, 0.0, field)], axis=0)
    field = dot(table[...], split(field, 0))
    return stacked(field[:half] + field[half:], lanes)


def fold(field):
    size = field.shape[1] // 2
    sign = jnp.where(lax.broadcasted_iota(jnp.int32, field.shape, 1) < size, 1.0, -1.0)
    return pltpu.roll(field, size, 1) + field * sign.astype(jnp.float32)


def solve(own, other, work, consts, ready=None):
    left, right, forth, back, pair, along = consts
    lanes = work.shape[1]
    size, half = lanes // 2, lanes // 4

    def across(field):
        field = dot(left[...], split(field, 0))
        return field[:size] + field[size:]

    def inner(field):
        field = dot(split(field, 1), right[...])
        return field[:, :lanes] + field[:, lanes:]

    for start in range(0, size, GROUP):
        rows = slice(start * half, (start + GROUP) * half)
        if ready is not None:
            ready(rows.start)
        field = own[rows, :].astype(jnp.float32) * other[rows, :].astype(jnp.float32)
        work[rows, :] = fold(middle(forth, spread(field, half), half))
    for start in range(0, half, GROUP):
        field = jnp.concatenate(
            [work[pl.ds(start + i, size, stride=half), :] for i in range(GROUP)], axis=1
        )
        field = inner(stacked(across(field), lanes))
        denom = jnp.concatenate(
            [along[...] + pair[start + i : start + i + 1, :] for i in range(GROUP)], axis=0
        )
        field = across(spread(inner(field / denom), size))
        for i in range(GROUP):
            work[pl.ds(start + i, size, stride=half), :] = field[:, i * lanes : (i + 1) * lanes]


def finished(work, other, back, start):
    half = work.shape[1] // 4
    rows = pl.ds(pl.multiple_of(start * half, GROUP * half), GROUP * half)
    field = middle(back, spread(fold(work[rows, :]), half), half)
    return rows, (field * other[rows, :].astype(jnp.float32)).astype(jnp.bfloat16)


def slot_kernel(slot, last, live, own, other, *refs):
    earlier, refs = refs[: 2 * last], refs[2 * last :]
    consts, out, work = refs[:6], refs[6], refs[7]
    solve(own, other, work, consts)
    for start in range(0, work.shape[1] // 2, GROUP):
        rows, term = finished(work, other, consts[3], start)
        term = jnp.where(live[slot] >= 0, term.astype(jnp.float32), 0.0)
        if last:
            total = earlier[0][rows, :].astype(jnp.float32) + earlier[1][rows, :].astype(jnp.float32)
            term = total + term
        out[rows, :] = term.astype(jnp.bfloat16)


def slot_term(slot, live, own, other, earlier, consts):
    vmem = pl.BlockSpec(memory_space=pltpu.VMEM)
    rows, lanes = own.shape
    return pl.pallas_call(
        functools.partial(slot_kernel, slot, 1 if earlier else 0),
        out_shape=jax.ShapeDtypeStruct(own.shape, jnp.bfloat16),
        in_specs=[pl.BlockSpec(memory_space=pltpu.SMEM)] + [vmem] * (2 + len(earlier) + len(consts)),
        out_specs=vmem,
        scratch_shapes=[pltpu.VMEM((rows, lanes), jnp.float32)],
        cost_estimate=pl.CostEstimate(
            flops=24 * rows * lanes * lanes * 8, bytes_accessed=6 * rows * lanes, transcendentals=0
        ),
        name=f"slot{slot}",
    )(live, own, other, *earlier, *consts)


def place(index):
    pairs = lax.axis_size("pair")
    return (index // pairs, index % pairs)


def whole_kernel(
    count, scale, live, orbital, *refs,
):
    consts, refs = refs[:6], refs[6:]
    total, phi, wide, own, other, terms, work, applied, slabs, sums, slot_sems, sent, came = refs
    slots, chunks = slot_sems.shape[1:]
    rows, lanes = slabs.shape[2:]
    band, pair = lax.axis_index("band"), lax.axis_index("pair")
    pairs = lax.axis_size("pair")
    me = band * pairs + pair
    last = slots - 1
    stride = 2**last
    side = lax.rem(band // stride, 2)

    def each(number, action):
        lax.fori_loop(1, number, lambda step, _: (action(step), 0)[1], 0)

    def peer_of(step):
        return lax.rem(me + step, count)

    def near(step):
        here = (band // (2 * stride) * stride + lax.rem(band, stride)) * pairs + pair
        at = lax.rem(here + step, count // 2)
        row = at // pairs
        row = row // stride * (2 * stride) + side * stride + lax.rem(row, stride)
        return row * pairs + lax.rem(at, pairs)

    def across(index):
        return index + (1 - 2 * side) * stride * pairs

    barrier = pltpu.get_barrier_semaphore()
    each(count, lambda step: pl.semaphore_signal(
        barrier, inc=1, device_id=place(peer_of(step)), device_id_type=MESH))
    grid = orbital[...].reshape(count * rows, lanes)
    own[...] = grid.reshape(count, rows, lanes)
    slabs[0, me] = own[me]
    pl.semaphore_wait(barrier, count - 1)

    def fetch(slot, chunk):
        far = 2**slot
        mate = band + far - 2 * far * lax.rem(band // far, 2)
        part = slice(chunk * count // chunks, (chunk + 1) * count // chunks)
        return pltpu.make_async_remote_copy(
            src_ref=own.at[part], dst_ref=other.at[slot, part],
            send_sem=slot_sems.at[0, slot, chunk], recv_sem=slot_sems.at[1, slot, chunk],
            device_id=(mate, pair), device_id_type=MESH,
        )

    def send(source, which, peer, origin, queue):
        return pltpu.make_async_remote_copy(
            src_ref=source.at[peer], dst_ref=slabs.at[which, origin],
            send_sem=sent.at[queue, peer], recv_sem=came.at[which, origin],
            device_id=place(peer), device_id_type=MESH,
        )

    def share(step):
        return pltpu.make_async_remote_copy(
            src_ref=sums.at[me], dst_ref=sums.at[me], send_sem=sent.at[2, step],
            recv_sem=came.at[2, step], device_id=place(peer_of(step)), device_id_type=MESH,
        )

    def widen(which, result):
        work[...] = slabs[which].reshape(count * rows, lanes).astype(jnp.float32)
        for row in range(rows):
            value = work[pl.ds(row, count, stride=rows), :]
            result[:, row * lanes : (row + 1) * lanes] = value.astype(result.dtype)

    fetches = [[fetch(slot, chunk) for chunk in range(chunks)] for slot in range(slots)]
    for copies in fetches:
        for copy in copies:
            copy.start()
    each(count // 2, lambda step: send(own, 0, near(step), me, 0).start())
    groups = lanes // 2 // GROUP
    blocks = count // groups
    flat = own.reshape(count * rows, lanes)
    for slot in range(slots):
        mate = other.at[slot].reshape(count * rows, lanes)

        def ready(row, slot=slot):
            chunk, rest = divmod(row, count * rows // chunks)
            if rest == 0:
                fetches[slot][chunk].wait()
                if slot == last and chunk == chunks - 1:
                    slabs[0, across(me)] = other[last, me]
                    each(count // 2, lambda step: send(
                        other.at[last], 0, near(step), across(me), 3).start())

        solve(flat, mate, work, consts, ready)
        for group in range(groups):
            if slot == last:
                group = lax.rem(me // blocks + groups // 2 + group, groups)
            span, term = finished(work, mate, consts[3], group * GROUP)
            term = jnp.where(live[0, slot] >= 0, term.astype(jnp.float32), 0.0)
            if slot < last:
                terms[slot, span, :] = term.astype(jnp.bfloat16)
                continue
            ahead = terms[0, span, :].astype(jnp.float32)
            for earlier in range(1, last):
                ahead = ahead + terms[earlier, span, :].astype(jnp.float32)
            ahead = (ahead + term).astype(jnp.bfloat16)
            applied[pl.ds(group * blocks, blocks)] = ahead.reshape(blocks, rows, lanes)
            for block in range(blocks):
                target = group * blocks + block

                @pl.when(target != me)
                def _(target=target):
                    send(applied, 1, target, me, 1).start()

    slabs[1, me] = applied[me]

    def arrived(step):
        send(own, 0, near(step), near(step), 0).wait()
        send(other.at[last], 0, near(step), across(near(step)), 3).wait()

    each(count // 2, arrived)
    widen(0, phi)
    each(count, lambda step: send(applied, 1, peer_of(step), peer_of(step), 1).wait())
    widen(1, wide)
    partial = lax.dot_general(
        phi[...], wide[...], (((1,), (1,)), ((), ())), preferred_element_type=jnp.float32
    ) * scale
    short = count * count // lanes
    sums[me] = jnp.concatenate(
        [partial[at : at + short] for at in range(0, count, short)], axis=1
    )
    each(count, lambda step: share(step).start())
    each(count, lambda step: share(step).wait())
    packed = jnp.sum(sums[...], axis=0)
    total[...] = jnp.concatenate(
        [packed[:, at : at + count] for at in range(0, lanes, count)], axis=0
    )


def projected(total, phi, applied):
    removed = lax.dot_general(
        total, phi.astype(jnp.float32), (((0,), (0,)), ((), ())), precision=lax.Precision.HIGHEST
    )
    return applied.astype(jnp.float32) - removed


def in_one_kernel(orbitals, partners, consts, count, lanes):
    cells = orbitals.shape[1]
    slots = partners.shape[1]
    slab = cells // count
    rows = slab // lanes
    vmem = pl.BlockSpec(memory_space=pltpu.VMEM)
    total, phi, wide = pl.pallas_call(
        functools.partial(whole_kernel, count, 1.0 / cells),
        out_shape=[
            jax.ShapeDtypeStruct((count, count), jnp.float32),
            jax.ShapeDtypeStruct((count, slab), jnp.bfloat16),
            jax.ShapeDtypeStruct((count, slab), jnp.bfloat16),
        ],
        in_specs=[pl.BlockSpec(memory_space=pltpu.SMEM)] + [vmem] * (1 + len(consts)),
        out_specs=[vmem] * 3,
        scratch_shapes=[
            pltpu.VMEM((count, rows, lanes), jnp.bfloat16),
            pltpu.VMEM((slots, count, rows, lanes), jnp.bfloat16),
            pltpu.VMEM((slots - 1, count * rows, lanes), jnp.bfloat16),
            pltpu.VMEM((count * rows, lanes), jnp.float32),
            pltpu.VMEM((count, rows, lanes), jnp.bfloat16),
            pltpu.VMEM((2, count, rows, lanes), jnp.bfloat16),
            pltpu.VMEM((count, count * count // lanes, lanes), jnp.float32),
            pltpu.SemaphoreType.DMA((2, slots, CHUNKS)),
            pltpu.SemaphoreType.DMA((4, count)),
            pltpu.SemaphoreType.DMA((3, count)),
        ],
        compiler_params=pltpu.CompilerParams(collective_id=0, has_side_effects=True),
        name="exchange",
    )(partners, orbitals, *consts)
    return projected(total, phi, wide)


def regrouped(value, count):
    bands, pairs = lax.axis_size("band"), lax.axis_size("pair")
    rows, lanes = value.shape
    value = value.reshape(bands, pairs, rows // count, lanes)
    value = lax.all_to_all(value, "band", split_axis=0, concat_axis=0, tiled=True)
    value = lax.all_to_all(value, "pair", split_axis=1, concat_axis=1, tiled=True)
    return value.reshape(count, rows * lanes // count)


def on_device(orbitals, partners):
    cells = orbitals.shape[1]
    size = round(cells ** (1.0 / 3.0))
    lanes = 2 * size
    count = lax.axis_size("band") * lax.axis_size("pair")
    consts = [jnp.asarray(table) for table in tables(size)]
    slab = cells // count
    small = count * count * count * 4 <= 2**24
    if small and slab % (8 * lanes) == 0 and count * count % (8 * lanes) == 0:
        return in_one_kernel(orbitals, partners, consts, count, lanes)
    own = orbitals.reshape(cells // lanes, lanes)
    live = partners[0]
    arrived = []
    for slot in range(partners.shape[1]):
        pairs = [(source, source ^ 2**slot) for source in range(lax.axis_size("band"))]
        arrived.append(lax.ppermute(own, "band", pairs))
    terms = []
    for slot in range(2):
        terms.append(slot_term(slot, live, own, arrived[slot], [], consts))
    applied = slot_term(2, live, own, arrived[2], terms, consts)
    phi, other = regrouped(own, count), regrouped(applied, count)
    partial = lax.dot_general(
        phi, other, (((1,), (1,)), ((), ())), preferred_element_type=jnp.float32
    )
    total = lax.psum(partial * (1.0 / cells), ("band", "pair"))
    return projected(total, phi, other)


def solution(mesh):
    placed = (P(("band", "pair"), None), P(("band", "pair"), None))
    return jax.shard_map(
        on_device, mesh=mesh, in_specs=placed, out_specs=P(None, ("band", "pair")), check_vma=False
    )
```

```python
import functools

import jax
import jax.numpy as jnp
import numpy as np
from jax import lax
from jax.experimental import pallas as pl
from jax.experimental.pallas import tpu as pltpu
from jax.sharding import PartitionSpec as P

screening = 0.05
GROUP = 8
CHUNKS = 4
MESH = pl.DeviceIdType.MESH


def halves(table):
    high = table.astype(np.float32).astype(jnp.bfloat16)
    low = (table - high.astype(np.float64)).astype(jnp.bfloat16)
    return np.asarray(high), np.asarray(low)


def tables(size):
    index = np.arange(size) + 1
    product = index[:, None] * index[None, :] % (2 * (size + 1))
    sine = np.sqrt(2.0 / (size + 1)) * np.sin(np.pi * product / (size + 1))
    half = size // 2
    high, low = halves(sine)
    left = np.block([[high, high], [low, low]])
    high, low = halves(np.kron(np.eye(2), sine))
    right = np.block([[high, low], [high, low]])
    even, odd = sine[:half, 0::2], sine[:half, 1::2]
    high, low = halves(np.concatenate([even, odd], axis=1))
    forth = np.block([[high, high], [low, low]])
    high, low = halves(np.concatenate([even.T, odd.T], axis=1))
    back = np.block([[high, high], [low, low]])
    lam = 2.0 - 2.0 * np.cos(np.pi * index / (size + 1))
    pair = np.concatenate(
        [lam[:half, None] + lam[None, :], lam[::-1][:half, None] + lam[None, :]], axis=1
    )
    pair = (pair + screening).astype(np.float32)
    along = np.broadcast_to(lam.astype(np.float32)[:, None], (size, 2 * size)).copy()
    return left, right, forth, back, pair, along


def split(value, axis):
    high = value.astype(jnp.bfloat16)
    low = (value - high.astype(jnp.float32)).astype(jnp.bfloat16)
    return jnp.concatenate([high, low], axis=axis)


def dot(a, b):
    return jnp.dot(a, b, preferred_element_type=jnp.float32)


def stacked(value, lanes):
    return jnp.concatenate(
        [value[:, at : at + lanes] for at in range(0, value.shape[1], lanes)], axis=0
    )


def spread(value, rows):
    return jnp.concatenate(
        [value[at : at + rows] for at in range(0, value.shape[0], rows)], axis=1
    )


def middle(table, field, half):
    lanes = 4 * half
    lane = lax.broadcasted_iota(jnp.int32, field.shape, 1) % lanes
    first = lane < 2 * half
    field = jnp.concatenate([jnp.where(first, field, 0.0), jnp.where(first, 0.0, field)], axis=0)
    field = dot(table[...], split(field, 0))
    return stacked(field[:half] + field[half:], lanes)


def fold(field):
    size = field.shape[1] // 2
    sign = jnp.where(lax.broadcasted_iota(jnp.int32, field.shape, 1) < size, 1.0, -1.0)
    return pltpu.roll(field, size, 1) + field * sign.astype(jnp.float32)


def solve(own, other, work, consts, ready=None):
    left, right, forth, back, pair, along = consts
    lanes = work.shape[1]
    size, half = lanes // 2, lanes // 4

    def across(field):
        field = dot(left[...], split(field, 0))
        return field[:size] + field[size:]

    def inner(field):
        field = dot(split(field, 1), right[...])
        return field[:, :lanes] + field[:, lanes:]

    for start in range(0, size, GROUP):
        rows = slice(start * half, (start + GROUP) * half)
        if ready is not None:
            ready(rows.start)
        field = own[rows, :].astype(jnp.float32) * other[rows, :].astype(jnp.float32)
        work[rows, :] = fold(middle(forth, spread(field, half), half))
    for start in range(0, half, GROUP):
        field = jnp.concatenate(
            [work[pl.ds(start + i, size, stride=half), :] for i in range(GROUP)], axis=1
        )
        field = inner(stacked(across(field), lanes))
        denom = jnp.concatenate(
            [along[...] + pair[start + i : start + i + 1, :] for i in range(GROUP)], axis=0
        )
        field = across(spread(inner(field / denom), size))
        for i in range(GROUP):
            work[pl.ds(start + i, size, stride=half), :] = field[:, i * lanes : (i + 1) * lanes]


def finished(work, other, back, start):
    half = work.shape[1] // 4
    rows = pl.ds(pl.multiple_of(start * half, GROUP * half), GROUP * half)
    field = middle(back, spread(fold(work[rows, :]), half), half)
    return rows, (field * other[rows, :].astype(jnp.float32)).astype(jnp.bfloat16)


def slot_kernel(slot, last, live, own, other, *refs):
    earlier, refs = refs[: 2 * last], refs[2 * last :]
    consts, out, work = refs[:6], refs[6], refs[7]
    solve(own, other, work, consts)
    for start in range(0, work.shape[1] // 2, GROUP):
        rows, term = finished(work, other, consts[3], start)
        term = jnp.where(live[slot] >= 0, term.astype(jnp.float32), 0.0)
        if last:
            total = earlier[0][rows, :].astype(jnp.float32) + earlier[1][rows, :].astype(jnp.float32)
            term = total + term
        out[rows, :] = term.astype(jnp.bfloat16)


def slot_term(slot, live, own, other, earlier, consts):
    vmem = pl.BlockSpec(memory_space=pltpu.VMEM)
    rows, lanes = own.shape
    return pl.pallas_call(
        functools.partial(slot_kernel, slot, 1 if earlier else 0),
        out_shape=jax.ShapeDtypeStruct(own.shape, jnp.bfloat16),
        in_specs=[pl.BlockSpec(memory_space=pltpu.SMEM)] + [vmem] * (2 + len(earlier) + len(consts)),
        out_specs=vmem,
        scratch_shapes=[pltpu.VMEM((rows, lanes), jnp.float32)],
        cost_estimate=pl.CostEstimate(
            flops=24 * rows * lanes * lanes * 8, bytes_accessed=6 * rows * lanes, transcendentals=0
        ),
        name=f"slot{slot}",
    )(live, own, other, *earlier, *consts)


def place(index):
    pairs = lax.axis_size("pair")
    return (index // pairs, index % pairs)


def whole_kernel(
    count, scale, live, orbital, *refs,
):
    consts, refs = refs[:6], refs[6:]
    total, phi, wide, own, other, terms, work, applied, slabs, sums, slot_sems, sent, came = refs
    slots, chunks = slot_sems.shape[1:]
    rows, lanes = slabs.shape[2:]
    band, pair = lax.axis_index("band"), lax.axis_index("pair")
    pairs = lax.axis_size("pair")
    me = band * pairs + pair
    last = slots - 1
    stride = 2**last
    side = lax.rem(band // stride, 2)

    def each(number, action):
        lax.fori_loop(1, number, lambda step, _: (action(step), 0)[1], 0)

    def peer_of(step):
        return lax.rem(me + step, count)

    def near(step):
        here = (band // (2 * stride) * stride + lax.rem(band, stride)) * pairs + pair
        at = lax.rem(here + step, count // 2)
        row = at // pairs
        row = row // stride * (2 * stride) + side * stride + lax.rem(row, stride)
        return row * pairs + lax.rem(at, pairs)

    def across(index):
        return index + (1 - 2 * side) * stride * pairs

    barrier = pltpu.get_barrier_semaphore()
    each(count, lambda step: pl.semaphore_signal(
        barrier, inc=1, device_id=place(peer_of(step)), device_id_type=MESH))
    grid = orbital[...].reshape(count * rows, lanes)
    own[...] = grid.reshape(count, rows, lanes)
    slabs[0, me] = own[me]
    pl.semaphore_wait(barrier, count - 1)

    def fetch(slot, chunk):
        far = 2**slot
        mate = band + far - 2 * far * lax.rem(band // far, 2)
        part = slice(chunk * count // chunks, (chunk + 1) * count // chunks)
        return pltpu.make_async_remote_copy(
            src_ref=own.at[part], dst_ref=other.at[slot, part],
            send_sem=slot_sems.at[0, slot, chunk], recv_sem=slot_sems.at[1, slot, chunk],
            device_id=(mate, pair), device_id_type=MESH,
        )

    def send(source, which, peer, origin, queue):
        return pltpu.make_async_remote_copy(
            src_ref=source.at[peer], dst_ref=slabs.at[which, origin],
            send_sem=sent.at[queue, peer], recv_sem=came.at[which, origin],
            device_id=place(peer), device_id_type=MESH,
        )

    def share(step):
        return pltpu.make_async_remote_copy(
            src_ref=sums.at[me], dst_ref=sums.at[me], send_sem=sent.at[2, step],
            recv_sem=came.at[2, step], device_id=place(peer_of(step)), device_id_type=MESH,
        )

    def widen(which, result):
        work[...] = slabs[which].reshape(count * rows, lanes).astype(jnp.float32)
        for row in range(rows):
            value = work[pl.ds(row, count, stride=rows), :]
            result[:, row * lanes : (row + 1) * lanes] = value.astype(result.dtype)

    fetches = [[fetch(slot, chunk) for chunk in range(chunks)] for slot in range(slots)]
    for copies in fetches:
        for copy in copies:
            copy.start()
    each(count // 2, lambda step: send(own, 0, near(step), me, 0).start())
    groups = lanes // 2 // GROUP
    blocks = count // groups
    flat = own.reshape(count * rows, lanes)
    for slot in range(slots):
        mate = other.at[slot].reshape(count * rows, lanes)

        def ready(row, slot=slot):
            chunk, rest = divmod(row, count * rows // chunks)
            if rest == 0:
                fetches[slot][chunk].wait()
                if slot == last and chunk == chunks - 1:
                    slabs[0, across(me)] = other[last, me]
                    each(count // 2, lambda step: send(
                        other.at[last], 0, near(step), across(me), 3).start())

        solve(flat, mate, work, consts, ready)
        for group in range(groups):
            if slot == last:
                group = lax.rem(me // blocks + groups // 2 + group, groups)
            span, term = finished(work, mate, consts[3], group * GROUP)
            term = jnp.where(live[0, slot] >= 0, term.astype(jnp.float32), 0.0)
            if slot < last:
                terms[slot, span, :] = term.astype(jnp.bfloat16)
                continue
            ahead = terms[0, span, :].astype(jnp.float32)
            for earlier in range(1, last):
                ahead = ahead + terms[earlier, span, :].astype(jnp.float32)
            ahead = (ahead + term).astype(jnp.bfloat16)
            applied[pl.ds(group * blocks, blocks)] = ahead.reshape(blocks, rows, lanes)
            for block in range(blocks):
                target = group * blocks + block

                @pl.when(target != me)
                def _(target=target):
                    send(applied, 1, target, me, 1).start()

    slabs[1, me] = applied[me]

    def arrived(step):
        send(own, 0, near(step), near(step), 0).wait()
        send(other.at[last], 0, near(step), across(near(step)), 3).wait()

    each(count // 2, arrived)
    widen(0, phi)
    each(count, lambda step: send(applied, 1, peer_of(step), peer_of(step), 1).wait())
    widen(1, wide)
    partial = lax.dot_general(
        phi[...], wide[...], (((1,), (1,)), ((), ())), preferred_element_type=jnp.float32
    ) * scale
    short = count * count // lanes
    sums[me] = jnp.concatenate(
        [partial[at : at + short] for at in range(0, count, short)], axis=1
    )
    each(count, lambda step: share(step).start())
    each(count, lambda step: share(step).wait())
    packed = jnp.sum(sums[...], axis=0)
    total[...] = jnp.concatenate(
        [packed[:, at : at + count] for at in range(0, lanes, count)], axis=0
    )


def projected(total, phi, applied):
    removed = lax.dot_general(
        total, phi.astype(jnp.float32), (((0,), (0,)), ((), ())), precision=lax.Precision.HIGH
    )
    return applied.astype(jnp.float32) - removed


def in_one_kernel(orbitals, partners, consts, count, lanes):
    cells = orbitals.shape[1]
    slots = partners.shape[1]
    slab = cells // count
    rows = slab // lanes
    vmem = pl.BlockSpec(memory_space=pltpu.VMEM)
    total, phi, wide = pl.pallas_call(
        functools.partial(whole_kernel, count, 1.0 / cells),
        out_shape=[
            jax.ShapeDtypeStruct((count, count), jnp.float32),
            jax.ShapeDtypeStruct((count, slab), jnp.bfloat16),
            jax.ShapeDtypeStruct((count, slab), jnp.bfloat16),
        ],
        in_specs=[pl.BlockSpec(memory_space=pltpu.SMEM)] + [vmem] * (1 + len(consts)),
        out_specs=[vmem] * 3,
        scratch_shapes=[
            pltpu.VMEM((count, rows, lanes), jnp.bfloat16),
            pltpu.VMEM((slots, count, rows, lanes), jnp.bfloat16),
            pltpu.VMEM((slots - 1, count * rows, lanes), jnp.bfloat16),
            pltpu.VMEM((count * rows, lanes), jnp.float32),
            pltpu.VMEM((count, rows, lanes), jnp.bfloat16),
            pltpu.VMEM((2, count, rows, lanes), jnp.bfloat16),
            pltpu.VMEM((count, count * count // lanes, lanes), jnp.float32),
            pltpu.SemaphoreType.DMA((2, slots, CHUNKS)),
            pltpu.SemaphoreType.DMA((4, count)),
            pltpu.SemaphoreType.DMA((3, count)),
        ],
        compiler_params=pltpu.CompilerParams(collective_id=0, has_side_effects=True),
        name="exchange",
    )(partners, orbitals, *consts)
    return projected(total, phi, wide)


def regrouped(value, count):
    bands, pairs = lax.axis_size("band"), lax.axis_size("pair")
    rows, lanes = value.shape
    value = value.reshape(bands, pairs, rows // count, lanes)
    value = lax.all_to_all(value, "band", split_axis=0, concat_axis=0, tiled=True)
    value = lax.all_to_all(value, "pair", split_axis=1, concat_axis=1, tiled=True)
    return value.reshape(count, rows * lanes // count)


def on_device(orbitals, partners):
    cells = orbitals.shape[1]
    size = round(cells ** (1.0 / 3.0))
    lanes = 2 * size
    count = lax.axis_size("band") * lax.axis_size("pair")
    consts = [jnp.asarray(table) for table in tables(size)]
    slab = cells // count
    small = count * count * count * 4 <= 2**24
    if small and slab % (8 * lanes) == 0 and count * count % (8 * lanes) == 0:
        return in_one_kernel(orbitals, partners, consts, count, lanes)
    own = orbitals.reshape(cells // lanes, lanes)
    live = partners[0]
    arrived = []
    for slot in range(partners.shape[1]):
        pairs = [(source, source ^ 2**slot) for source in range(lax.axis_size("band"))]
        arrived.append(lax.ppermute(own, "band", pairs))
    terms = []
    for slot in range(2):
        terms.append(slot_term(slot, live, own, arrived[slot], [], consts))
    applied = slot_term(2, live, own, arrived[2], terms, consts)
    phi, other = regrouped(own, count), regrouped(applied, count)
    partial = lax.dot_general(
        phi, other, (((1,), (1,)), ((), ())), preferred_element_type=jnp.float32
    )
    total = lax.psum(partial * (1.0 / cells), ("band", "pair"))
    return projected(total, phi, other)


def solution(mesh):
    placed = (P(("band", "pair"), None), P(("band", "pair"), None))
    return jax.shard_map(
        on_device, mesh=mesh, in_specs=placed, out_specs=P(None, ("band", "pair")), check_vma=False
    )
```
